32 devices in a mesh: tm: 4 (over y, x), view: 8 (over z, core).
Axes of the slice: x: 2, y: 2, z: 4, core: 2. Of those that a mesh axis runs over, the one named last changes fastest.
Arguments:
- tokens: bfloat16 [8, 8, 256, 2048], P('view', 'tm'), may hold values from -6 to 6
- spatial_q: bfloat16 [8, 8, 256, 2048], P('view', 'tm'), may hold values from -5 to 5
- spatial_k: bfloat16 [8, 8, 256, 2048], P('view', 'tm'), may hold values from -100 to 100
- spatial_v: bfloat16 [8, 8, 256, 2048], P('view', 'tm'), may hold values from -6 to 6
- norm_gain: bfloat16 [2048], replicated, may hold values from 0.099609375 to 1.8984375
- w_query: bfloat16 [2048, 1024], P('view', 'tm'), as said below
- w_key: bfloat16 [2048, 1024], P('view', 'tm')
- w_value: bfloat16 [2048, 1024], P('view', 'tm'), may hold values from -0.125 to 0.125
- counts: int32 [8], P('view'), may hold values from 1 to 8, as said below
Outputs:
- mixed: bfloat16 [8, 8, 256, 2048], P('view', 'tm')
- attended: bfloat16 [8, 8, 256, 1024], P('view', 'tm')
The draws below stay inside these ranges and needn't reach their ends.
Inputs may be any that keep to these rules, and one draw needn't show every extreme that they name: `w_query`: every entry has magnitude at most 5 · 2048 ** -0.5 (about 0.1105). counts[s] + counts[s + 4] = 9 for every s below 4.
All inputs are finite; a program needn't handle non-finite values.
Results may differ from the reference program's by a relative error of at most 0.0075.
Values may be sent and summed in bfloat16 or wider, within the bound.
No kernel may reach another device: no remote copies, remote signals or barrier semaphores. Data moves between devices by JAX's collectives and lax.ppermute only.
A program may use at most 128 MiB of HBM per device.

```python
import jax
import jax.numpy as jnp
from jax import lax

D = 2048
H = 16
HD = 128
HT = 8
P_SIZE = 256
FRAMES = 8
STREAMS = 8
DT = 1024


def spatial_pair(key):
    base = jax.random.fold_in(key, 101)
    key_query, key_keys = jax.random.split(base, 2)
    full_shape = (STREAMS, FRAMES, P_SIZE, D)
    queries = jnp.clip(jax.random.normal(key_query, full_shape, jnp.float32), -5.0, 5.0)
    keys = jnp.clip(jax.random.normal(key_keys, full_shape, jnp.float32), -5.0, 5.0)
    return (queries, keys)


def draw_spatial_q(key, part):
    return spatial_pair(key)[0].astype(jnp.bfloat16)


def draw_spatial_k(key, part):
    return spatial_pair(key)[1].astype(jnp.bfloat16)


def draw_tokens(key, part):
    key_noise = jax.random.fold_in(jax.random.fold_in(key, 202), 1)
    full_shape = (STREAMS, FRAMES, P_SIZE, D)
    values = jax.random.normal(key_noise, full_shape, jnp.float32)
    return jnp.clip(values, -6.0, 6.0).astype(jnp.bfloat16)


def weight_pair(key):
    key_query, key_keys = jax.random.split(jax.random.fold_in(key, 303), 2)
    query_weight = jnp.clip(jax.random.normal(key_query, (D, DT), jnp.float32), -5.0, 5.0) * D ** (-0.5)
    key_weight = jnp.clip(jax.random.normal(key_keys, (D, DT), jnp.float32), -5.0, 5.0) * D ** (-0.5)
    return (query_weight, key_weight)


def draw_w_query(key, part):
    return weight_pair(key)[0].astype(jnp.bfloat16)


def draw_w_key(key, part):
    return weight_pair(key)[1].astype(jnp.bfloat16)


def draw_counts(key, part):
    half_streams = STREAMS // 2
    first = jax.random.randint(jax.random.fold_in(key, 404), (half_streams,), 1, FRAMES + 1, jnp.int32)
    first = first.at[0].set(FRAMES)
    return jnp.concatenate([first, FRAMES + 1 - first]).astype(jnp.int32)


def steps_of(key, shape, shards, smallest, high):
    gain = 1.0
    for axis_at, shards_of in shards:
        draws = jax.random.uniform(jax.random.fold_in(jax.random.fold_in(key, 6), axis_at), (shards_of,), jnp.float32, smallest / len(shards), high / len(shards))
        gain = gain * jnp.repeat(jnp.exp(draws), shape[axis_at] // shards_of).reshape((-1,) + (1,) * (len(shape) - 1 - axis_at))
    return gain


def scatter_about(stream_key, dims, scale, most, pieces=(), kind=jnp.bfloat16):
    entries = jax.random.normal(stream_key, dims, jnp.float32) * scale
    if len(pieces) > 0:
        entries = steps_of(stream_key, dims, pieces, -0.22, 0.18) * entries
    return jnp.clip(entries, min=-most, max=most).astype(kind)


def setup_inputs(seed: int = 0) -> dict:
    seeds = jax.random.split(jax.random.key(seed), 10)
    tokens = draw_tokens(jax.random.fold_in(seeds[9], 71), 0)
    spatial_q = draw_spatial_q(jax.random.fold_in(seeds[9], 71), 0)
    spatial_k = draw_spatial_k(jax.random.fold_in(seeds[9], 71), 0)
    spatial_v = scatter_about(seeds[3], (STREAMS, FRAMES, P_SIZE, D), 1.0, 6.0, ((0, 8), (1, 4)))
    norm_gain = jnp.clip(1.0 + 0.18 * jax.random.normal(seeds[4], (D,), jnp.float32), 0.099609375, 1.8984375).astype(jnp.bfloat16)
    w_query = draw_w_query(jax.random.fold_in(seeds[9], 71), 0)
    w_key = draw_w_key(jax.random.fold_in(seeds[9], 71), 0)
    w_value = scatter_about(seeds[7], (D, DT), D ** -0.5, 0.125, ((0, 8), (1, 4)))
    counts = draw_counts(jax.random.fold_in(seeds[9], 71), 0)
    return {"tokens": tokens, "spatial_q": spatial_q, "spatial_k": spatial_k, "spatial_v": spatial_v, "norm_gain": norm_gain, "w_query": w_query, "w_key": w_key, "w_value": w_value, "counts": counts}


FILL_VALUE = -1e+30
EPSILON = 1e-06

def spatial_stream(tokens, spatial_q, spatial_k, spatial_v):
    frames = tokens.shape[0]
    head_shape = (frames, P_SIZE, H, HD)
    query_heads = spatial_q.reshape(head_shape).astype(jnp.float32)
    key_heads = spatial_k.reshape(head_shape).astype(jnp.float32)
    value_heads = spatial_v.reshape(head_shape).astype(jnp.float32)
    scores = jnp.einsum('fphd,fqhd->fhpq', query_heads, key_heads) * HD ** (-0.5)
    row_top = lax.optimization_barrier(jnp.max(scores, axis=-1, keepdims=True))
    exponent = jnp.exp(scores - row_top)
    row_total = lax.optimization_barrier(jnp.sum(exponent, axis=-1))
    weights = lax.optimization_barrier(exponent.astype(jnp.bfloat16)).astype(jnp.float32)
    summed = jnp.einsum('fhpq,fqhd->fphd', weights, value_heads)
    result = summed / jnp.transpose(row_total, (0, 2, 1))[..., None]
    return (tokens.astype(jnp.float32) + result.reshape(frames, P_SIZE, D)).astype(jnp.bfloat16)

def temporal_stream(mixed, norm_gain, w_query, w_key, w_value, length):
    frames = mixed.shape[0]
    wide = mixed.astype(jnp.float32)
    scaled = wide * lax.rsqrt(lax.optimization_barrier(jnp.mean(wide * wide, axis=-1, keepdims=True)) + EPSILON)
    normed = (scaled * norm_gain.astype(jnp.float32)).astype(jnp.bfloat16)
    token_rows = normed.reshape(frames * P_SIZE, D)
    head_shape = (frames, P_SIZE, HT, HD)
    query_heads = jnp.dot(token_rows, w_query, preferred_element_type=jnp.float32).astype(jnp.bfloat16)
    key_heads = jnp.dot(token_rows, w_key, preferred_element_type=jnp.float32).astype(jnp.bfloat16)
    value_heads = jnp.dot(token_rows, w_value, preferred_element_type=jnp.float32).astype(jnp.bfloat16)
    query_heads = query_heads.reshape(head_shape).astype(jnp.float32)
    key_heads = key_heads.reshape(head_shape).astype(jnp.float32)
    value_heads = value_heads.reshape(head_shape).astype(jnp.float32)
    scores = jnp.einsum('fphd,gphd->fphg', query_heads, key_heads) * HD ** (-0.5)
    frame_pos = jnp.arange(frames, dtype=jnp.int32)
    causal = (frame_pos[None, :] <= frame_pos[:, None])[:, None, None, :]
    masked = jnp.where(causal, scores, FILL_VALUE)
    row_top = lax.optimization_barrier(jnp.max(masked, axis=-1, keepdims=True))
    exponent = jnp.where(causal, jnp.exp(masked - row_top), 0.0)
    row_total = lax.optimization_barrier(jnp.sum(exponent, axis=-1))
    weights = lax.optimization_barrier(exponent.astype(jnp.bfloat16)).astype(jnp.float32)
    result = jnp.einsum('fphg,gphd->fphd', weights, value_heads) / row_total[..., None]
    live = (frame_pos < length)[:, None, None, None]
    result = jnp.where(live, result, 0.0)
    return result.reshape(frames, P_SIZE, HT * HD).astype(jnp.bfloat16)

def reference(tokens, spatial_q, spatial_k, spatial_v, norm_gain, w_query, w_key, w_value, counts):

    def one_stream(packed):
        stream_tokens, stream_q, stream_k, stream_v, length = packed
        mixed = spatial_stream(stream_tokens, stream_q, stream_k, stream_v)
        attended = temporal_stream(mixed, norm_gain, w_query, w_key, w_value, length)
        return (mixed, attended)
    mixed, attended = lax.map(one_stream, (tokens, spatial_q, spatial_k, spatial_v, counts))
    return (mixed, attended)
```

```python
import functools
import math

import jax
import jax.numpy as jnp
from jax import lax
from jax.experimental import pallas as pl
from jax.experimental.pallas import tpu as pltpu
from jax.sharding import PartitionSpec as P

HD = 128
LANES = 128
FILL_VALUE = -1e30
EPSILON = 1e-06
CHUNKS = 2
TILE = 32
SCALE = HD ** (-0.5) * math.log2(math.e)


def softmax_parts(scores):
    top = jnp.max(scores, axis=-1, keepdims=True)
    exponent = jnp.exp2((scores - top) * SCALE)
    return exponent.astype(jnp.bfloat16), jnp.sum(exponent, axis=-1, keepdims=True)


def times_transposed(a, b):
    return lax.dot_general(a, b, (((1,), (1,)), ((), ())), preferred_element_type=jnp.float32)


def spatial_body(chunks, half_ref, tok_ref, q_ref, k_ref, v_ref, gain_ref, mixed_ref, *outs):
    rows, width = q_ref.shape
    squares = jnp.zeros((rows, HD), jnp.float32)
    for h in range(width // HD):
        cols = slice(h * HD, (h + 1) * HD)
        weights, total = softmax_parts(times_transposed(q_ref[:, cols], k_ref[:, cols]))
        summed = jnp.dot(weights, v_ref[:, cols], preferred_element_type=jnp.float32)
        mixed = (tok_ref[:, cols].astype(jnp.float32) + summed / total).astype(jnp.bfloat16)
        mixed_ref[:, cols] = mixed
        wide = mixed.astype(jnp.float32)
        squares = squares + wide * wide
    inverse = lax.rsqrt(jnp.sum(squares, axis=-1, keepdims=True) / width + EPSILON)
    wide = mixed_ref[...].astype(jnp.float32)
    normed = (wide * inverse * gain_ref[...].astype(jnp.float32)).astype(jnp.bfloat16)
    step = rows // (2 * chunks)
    for low in range(2):

        @pl.when(half_ref[0] == low)
        def _():
            for side in range(2):
                for c in range(chunks):
                    start = ((low + side) % 2 * chunks + c) * step
                    outs[side * chunks + c][...] = normed[start : start + step]


def spatial_call(half, tokens, q, k, v, gain, chunks):
    _, frames, size, width = tokens.shape
    full = pl.BlockSpec((None, None, size, width), lambda f, at: (0, f, 0, 0))
    step = size // (2 * chunks)
    piece = pl.BlockSpec((None, step, width), lambda f, at: (f, 0, 0))
    elements = frames * size * width
    outs = pl.pallas_call(
        functools.partial(spatial_body, chunks),
        grid_spec=pltpu.PrefetchScalarGridSpec(
            num_scalar_prefetch=1,
            grid=(frames,),
            in_specs=[full] * 4 + [pl.BlockSpec((1, width), lambda f, at: (0, 0))],
            out_specs=[full] + [piece] * (2 * chunks),
        ),
        out_shape=[jax.ShapeDtypeStruct(tokens.shape, jnp.bfloat16)]
        + [jax.ShapeDtypeStruct((frames, step, width), jnp.bfloat16)] * (2 * chunks),
        cost_estimate=pl.CostEstimate(
            flops=4 * elements * size, bytes_accessed=12 * elements, transcendentals=elements * size // HD
        ),
        name="spatial",
    )(half, tokens, q, k, v, gain.reshape(1, width))
    return outs[0], outs[1 : 1 + chunks], outs[1 + chunks :]


def temporal_body(pieces, counts, tile, place_ref, live_ref, *refs):
    blocks = sum(counts)
    xs, ws = refs[:pieces], refs[pieces : pieces + blocks]
    outs = refs[pieces + blocks : 2 * pieces + blocks]
    w_all, x_all, qkv, w_sem, x_sem = refs[2 * pieces + blocks :]
    frames, rows, width = xs[0].shape
    kinds, depth, cols = ws[0].shape
    me, length = place_ref[0], live_ref[0]

    def w_copy(n, kind, i):
        source = ws[sum(counts[:n]) + i].at[kind]
        start = pl.multiple_of(place_ref[1 + i] * depth, depth)
        return pltpu.make_async_copy(source, w_all.at[n, kind, pl.ds(start, depth)], w_sem.at[n, kind, i])

    def x_copy(g):
        return pltpu.make_async_copy(xs[g], x_all.at[g], x_sem.at[g])

    x_copy(0).start()
    order = [(n, kind) for n in range(len(counts)) for kind in range(kinds)]
    for n, kind in order:
        for i in range(counts[n]):
            w_copy(n, kind, i).start()
        if n == 0 and kind + 1 < pieces:
            x_copy(kind + 1).start()
    for g in range(kinds + 1, pieces):
        x_copy(g).start()
    for g in range(pieces):
        x_copy(g).wait()
        x = x_all[g].reshape(frames * rows, width)
        for n, kind in order:
            if g == 0:
                for i in range(counts[n]):
                    w_copy(n, kind, i).wait()
            part = jnp.dot(x, w_all[n, kind], preferred_element_type=jnp.float32)
            qkv[n, kind, g] = part.astype(jnp.bfloat16).reshape(frames, rows, cols)

    size = pieces * frames * tile
    row = lax.broadcasted_iota(jnp.int32, (size, size), 0)
    col = lax.broadcasted_iota(jnp.int32, (size, size), 1)

    def frame_of(a):
        return jnp.bitwise_xor(a // (frames * tile), me) * frames + (a // tile) % frames

    seen = (row % tile == col % tile) & (frame_of(col) <= frame_of(row))
    live = frame_of(lax.broadcasted_iota(jnp.int32, (size, HD), 0)) < length
    for p in range(rows // tile):
        at = slice(p * tile, (p + 1) * tile)
        for n in range(len(counts)):
            for h in range(cols // HD):
                here = slice(h * HD, (h + 1) * HD)
                q, k, v = (qkv[n, kind, :, :, at, here].reshape(size, HD) for kind in range(3))
                weights, total = softmax_parts(jnp.where(seen, times_transposed(q, k), FILL_VALUE))
                result = jnp.dot(weights, v, preferred_element_type=jnp.float32) / total
                result = jnp.where(live, result, 0.0).astype(jnp.bfloat16).reshape(pieces, frames, tile, HD)
                there = slice(n * cols + h * HD, n * cols + (h + 1) * HD)
                for g in range(pieces):
                    outs[g][:, at, there] = result[g]


def temporal_call(place, live, xs, groups):
    frames, rows, width = xs[0].shape
    kinds, depth, cols = groups[0][0].shape
    counts = tuple(len(blocks) for blocks in groups)
    pieces = len(xs)
    whole = pl.BlockSpec(memory_space=pltpu.VMEM)
    total = pieces * frames * rows
    out = jax.ShapeDtypeStruct((frames, rows, len(groups) * cols), jnp.bfloat16)
    return pl.pallas_call(
        functools.partial(temporal_body, pieces, counts, min(TILE, rows)),
        grid_spec=pltpu.PrefetchScalarGridSpec(
            num_scalar_prefetch=2,
            grid=(),
            in_specs=[pl.BlockSpec(memory_space=pl.ANY)] * (sum(counts) + pieces),
            out_specs=[whole] * pieces,
            scratch_shapes=[
                pltpu.VMEM((len(groups), kinds, counts[0] * depth, cols), jnp.bfloat16),
                pltpu.VMEM((pieces, frames, rows, width), jnp.bfloat16),
                pltpu.VMEM((len(groups), kinds, pieces, frames, rows, cols), jnp.bfloat16),
                pltpu.SemaphoreType.DMA((len(groups), kinds, counts[0])),
                pltpu.SemaphoreType.DMA((pieces,)),
            ],
        ),
        out_shape=[out] * pieces,
        cost_estimate=pl.CostEstimate(
            flops=2 * total * width * kinds * cols * len(groups),
            bytes_accessed=2 * (total * width + kinds * width * cols * len(groups)),
            transcendentals=0,
        ),
        name="temporal",
    )(place, live, *xs, *[block for blocks in groups for block in blocks])


def place_body(width, me_ref, *refs):
    out_ref = refs[-1]
    parts = refs[:-1]
    pieces = out_ref.shape[2] // width
    chunks = len(parts) // pieces
    frames, rows, _ = parts[0].shape
    for c in range(chunks):
        for g in range(pieces):
            owner = jnp.bitwise_xor(me_ref[0], g)
            start = pl.multiple_of((owner % 2 * chunks + c) * rows, rows)
            for n in range(parts[0].shape[2] // width):
                col = pl.multiple_of(jnp.bitwise_xor(owner, n) * width, width)
                out_ref[:, pl.ds(start, rows), pl.ds(col, width)] = parts[c * pieces + g][:, :, n * width : (n + 1) * width]


def place_call(me, parts, frames, size, width, columns):
    whole = pl.BlockSpec(memory_space=pltpu.VMEM)
    return pl.pallas_call(
        functools.partial(place_body, width),
        grid_spec=pltpu.PrefetchScalarGridSpec(
            num_scalar_prefetch=1, grid=(), in_specs=[whole] * len(parts), out_specs=whole
        ),
        out_shape=jax.ShapeDtypeStruct((frames, size, columns), jnp.bfloat16),
        cost_estimate=pl.CostEstimate(flops=0, bytes_accessed=4 * frames * size * columns, transcendentals=0),
        name="place",
    )(me, *parts)


def flip(x, bit, n_tm):
    return lax.ppermute(x, "tm", [(i, i ^ bit) for i in range(n_tm)])


def gather_blocks(block, n_view):
    depth = block.shape[1]
    if depth % LANES or n_view % 2:
        return [lax.all_gather(block, "view", axis=1, tiled=True)]
    mine = [block]
    for _ in range(n_view // 2 - 1):
        mine.append(lax.ppermute(mine[-1], "view", [(i, (i + 2) % n_view) for i in range(n_view)]))
    swap = [(i, i ^ 1) for i in range(n_view)]
    return mine + [lax.ppermute(b, "view", swap) for b in mine]


def shards(n_tm, n_view, tokens, spatial_q, spatial_k, spatial_v, norm_gain, w_query, w_key, w_value, counts):
    me = lax.axis_index("tm").astype(jnp.int32)
    view = lax.axis_index("view").astype(jnp.int32)
    _, frames, size, _ = tokens.shape
    width = w_query.shape[1]

    own_w = jnp.stack([w_query, w_key, w_value])
    near_w = flip(own_w, 1, n_tm)
    own_blocks = gather_blocks(own_w, n_view)
    near_w, _ = lax.optimization_barrier((near_w, own_blocks[len(own_blocks) // 2 - 1]))
    near_blocks = gather_blocks(near_w, n_view)
    if len(own_blocks) == 1:
        place = [me, jnp.int32(0)]
    else:
        ring = n_view // 2
        place = [me] + [(view - 2 * k) % n_view for k in range(ring)]
        place += [((view ^ 1) - 2 * k) % n_view for k in range(ring)]
    place = jnp.stack(place).astype(jnp.int32)

    mixed, own, away = spatial_call(
        (me % 2).reshape(1), tokens, spatial_q, spatial_k, spatial_v, norm_gain, CHUNKS
    )
    near = [flip(a, 1, n_tm) for a in away]
    far = [flip(a, 2, n_tm) for a in own]
    across = [flip(a, 2, n_tm) for a in near]
    parts = []
    for c in range(CHUNKS):
        outs = temporal_call(place, counts, [own[c], near[c], far[c], across[c]], [own_blocks, near_blocks])
        parts += [outs[0]] + [flip(outs[g], g, n_tm) for g in range(1, 4)]
    attended = place_call(me.reshape(1), parts, frames, size, width, n_tm * width)
    return (mixed, attended.reshape((1,) + attended.shape))


def solution(mesh):
    rows = P("view", "tm", None, None)
    in_specs = (rows, rows, rows, rows, P(), P("view", "tm"), P("view", "tm"), P("view", "tm"), P("view"))
    body = functools.partial(shards, mesh.shape["tm"], mesh.shape["view"])
    return jax.shard_map(body, mesh=mesh, in_specs=in_specs, out_specs=(rows, rows), check_vma=False)
```

```python
import functools
import math

import jax
import jax.numpy as jnp
from jax import lax
from jax.experimental import pallas as pl
from jax.experimental.pallas import tpu as pltpu
from jax.sharding import PartitionSpec as P


HD = 128
LANES = 128
FILL_VALUE = -1e30
EPSILON = 1e-06
CHUNKS = 2
TILE = 32
VMEM_LIMIT = 24 * 2**20
SPLIT = (0,)
SCALE = HD ** (-0.5) * math.log2(math.e)


def softmax_parts(scores):
    top = jnp.max(scores, axis=-1, keepdims=True)
    exponent = jnp.exp2((scores - top) * SCALE)
    return exponent.astype(jnp.bfloat16), jnp.sum(exponent, axis=-1, keepdims=True)


def times_transposed(a, b):
    return lax.dot_general(a, b, (((1,), (1,)), ((), ())), preferred_element_type=jnp.float32)


def spatial_body(chunks, half_ref, tok_ref, q_ref, k_ref, v_ref, gain_ref, *refs):
    mixed_ref, *outs = refs[-1 - chunks :]
    rows, width = q_ref.shape
    squares = jnp.zeros((rows, HD), jnp.float32)
    for h in range(width // HD):
        cols = slice(h * HD, (h + 1) * HD)
        weights, total = softmax_parts(times_transposed(q_ref[:, cols], k_ref[:, cols]))
        summed = jnp.dot(weights, v_ref[:, cols], preferred_element_type=jnp.float32)
        mixed = (tok_ref[:, cols].astype(jnp.float32) + summed / total).astype(jnp.bfloat16)
        mixed_ref[:, cols] = mixed
        wide = mixed.astype(jnp.float32)
        squares = squares + wide * wide
    inverse = lax.rsqrt(jnp.sum(squares, axis=-1, keepdims=True) / width + EPSILON)
    wide = mixed_ref[...].astype(jnp.float32)
    normed = (wide * inverse * gain_ref[...].astype(jnp.float32)).astype(jnp.bfloat16)
    step = rows // chunks
    for c in range(chunks):
        outs[c][...] = normed[c * step : (c + 1) * step]


def spatial_call(half, tokens, q, k, v, gain, before, chunks):
    _, frames, size, width = tokens.shape
    rows = size // 2
    some = pl.BlockSpec((None, None, rows, width), lambda f, at: (0, f, at[0], 0))
    full = pl.BlockSpec((None, None, size, width), lambda f, at: (0, f, 0, 0))
    piece = pl.BlockSpec((None, rows // chunks, width), lambda f, at: (f, 0, 0))
    elements = frames * rows * width
    ins = [some, some, full, full, pl.BlockSpec((1, width), lambda f, at: (0, 0))]
    args = [half, tokens, q, k, v, gain.reshape(1, width)]
    if before is not None:
        ins.append(pl.BlockSpec(memory_space=pl.ANY))
        args.append(before)
    outs = pl.pallas_call(
        functools.partial(spatial_body, chunks),
        grid_spec=pltpu.PrefetchScalarGridSpec(
            num_scalar_prefetch=1, grid=(frames,), in_specs=ins, out_specs=[some] + [piece] * chunks
        ),
        out_shape=[jax.ShapeDtypeStruct(tokens.shape, jnp.bfloat16)]
        + [jax.ShapeDtypeStruct((frames, rows // chunks, width), jnp.bfloat16)] * chunks,
        input_output_aliases={} if before is None else {6: 0},
        cost_estimate=pl.CostEstimate(
            flops=4 * elements * size, bytes_accessed=16 * elements, transcendentals=elements * size // HD
        ),
        name="spatial",
    )(*args)
    return outs[0], outs[1:]


def temporal_body(pieces, groups, tile, place_ref, live_ref, *refs):
    xs, refs = refs[:pieces], refs[pieces:]
    *refs, qkv = refs
    outs, refs = refs[-pieces:], refs[:-pieces]
    frames, rows, width = xs[0].shape
    kinds, depth, cols = refs[0].shape
    blocks = width // depth
    ws, early = refs[: groups * blocks], refs[groups * blocks :]
    me, length = place_ref[0], live_ref[0]
    for n in range(groups):
        for kind in range(kinds):
            for g in range(pieces):
                part = None
                for i in range(blocks):
                    start = pl.multiple_of(place_ref[1 + i] * depth, depth)
                    x = xs[g][:, :, pl.ds(start, depth)].reshape(frames * rows, depth)
                    more = jnp.dot(x, ws[n * blocks + i][kind], preferred_element_type=jnp.float32)
                    part = more if part is None else part + more
                qkv[n, kind, g] = part.astype(jnp.bfloat16).reshape(frames, rows, cols)

    size = pieces * frames * tile
    row = lax.broadcasted_iota(jnp.int32, (size, size), 0)
    col = lax.broadcasted_iota(jnp.int32, (size, size), 1)

    def frame_of(a):
        return jnp.bitwise_xor(a // (frames * tile), me) * frames + (a // tile) % frames

    seen = (row % tile == col % tile) & (frame_of(col) <= frame_of(row))
    live = frame_of(lax.broadcasted_iota(jnp.int32, (size, HD), 0)) < length
    first = outs[0].shape[2] - groups * cols
    for g, ref in enumerate(early):
        outs[g][:, :, :first] = ref[...]
    for p in range(rows // tile):
        at = slice(p * tile, (p + 1) * tile)
        for n in range(groups):
            for h in range(cols // HD):
                here = slice(h * HD, (h + 1) * HD)
                q, k, v = (qkv[n, kind, :, :, at, here].reshape(size, HD) for kind in range(3))
                weights, total = softmax_parts(jnp.where(seen, times_transposed(q, k), FILL_VALUE))
                result = jnp.dot(weights, v, preferred_element_type=jnp.float32) / total
                result = jnp.where(live, result, 0.0).astype(jnp.bfloat16).reshape(pieces, frames, tile, HD)
                there = first + n * cols + h * HD
                for g in range(pieces):
                    outs[g][:, at, there : there + HD] = result[g]


def temporal_call(place, live, xs, ws, early):
    frames, rows, width = xs[0].shape
    kinds, depth, cols = ws[0].shape
    pieces, groups = len(xs), len(ws) * depth // width
    whole = pl.BlockSpec(memory_space=pltpu.VMEM)
    total = pieces * frames * rows
    out = jax.ShapeDtypeStruct((frames, rows, (groups + (1 if early else 0)) * cols), jnp.bfloat16)
    return pl.pallas_call(
        functools.partial(temporal_body, pieces, groups, min(TILE, rows)),
        grid_spec=pltpu.PrefetchScalarGridSpec(
            num_scalar_prefetch=2,
            grid=(),
            in_specs=[whole] * (len(ws) + pieces + len(early)),
            out_specs=[whole] * pieces,
            scratch_shapes=[pltpu.VMEM((groups, kinds, pieces, frames, rows, cols), jnp.bfloat16)],
        ),
        out_shape=[out] * pieces,
        compiler_params=pltpu.CompilerParams(vmem_limit_bytes=VMEM_LIMIT),
        cost_estimate=pl.CostEstimate(
            flops=2 * total * width * kinds * cols * groups,
            bytes_accessed=2 * (total * width + kinds * width * cols * groups),
            transcendentals=0,
        ),
        name="temporal",
    )(place, live, *xs, *ws, *early)


def place_body(c, chunks, width, me_ref, *refs):
    *parts, out_ref, sems = refs
    pieces = out_ref.shape[2] // width
    parts = parts[:pieces]
    rows = parts[0].shape[1]
    copies = []
    for g, part in enumerate(parts):
        owner = jnp.bitwise_xor(me_ref[0], g)
        start = pl.multiple_of((owner % 2 * chunks + c) * rows, rows)
        for n in range(part.shape[2] // width):
            col = pl.multiple_of(jnp.bitwise_xor(owner, n) * width, width)
            target = out_ref.at[:, pl.ds(start, rows), pl.ds(col, width)]
            copies.append(pltpu.make_async_copy(part.at[:, :, pl.ds(n * width, width)], target, sems.at[g, n]))
    for copy in copies:
        copy.start()
    for copy in copies:
        copy.wait()


def place_call(me, parts, before, c, chunks, size, width, columns):
    anywhere = pl.BlockSpec(memory_space=pl.ANY)
    frames, _, cols = parts[0].shape
    before = [] if before is None else [before]
    return pl.pallas_call(
        functools.partial(place_body, c, chunks, width),
        grid_spec=pltpu.PrefetchScalarGridSpec(
            num_scalar_prefetch=1,
            grid=(),
            in_specs=[pl.BlockSpec(memory_space=pltpu.VMEM)] * len(parts) + [anywhere] * len(before),
            out_specs=anywhere,
            scratch_shapes=[pltpu.SemaphoreType.DMA((len(parts), cols // width))],
        ),
        out_shape=jax.ShapeDtypeStruct((frames, size, columns), jnp.bfloat16),
        input_output_aliases={1 + len(parts): 0} if before else {},
        compiler_params=pltpu.CompilerParams(vmem_limit_bytes=VMEM_LIMIT),
        name="place",
    )(me, *parts, *before)


def flip(x, bit, n_tm):
    return lax.ppermute(x, "tm", [(i, i ^ bit) for i in range(n_tm)])


def after(x, *others):
    return lax.optimization_barrier((x,) + others)[0]


def shards(n_tm, n_view, tokens, spatial_q, spatial_k, spatial_v, norm_gain, w_query, w_key, w_value, counts):
    me = lax.axis_index("tm").astype(jnp.int32)
    view = lax.axis_index("view").astype(jnp.int32)
    _, _, size, _ = tokens.shape
    depth, width = w_query.shape
    swap = [(i, i ^ 1) for i in range(n_view)]
    ring = [(i, (i + 2) % n_view) for i in range(n_view)]
    by_ring = depth % LANES == 0 and n_view == 8

    def cross(x, bit):
        return flip(x, bit, n_tm)

    def turn(x):
        return lax.ppermute(x, "view", ring)

    own_w = jnp.stack([w_query, w_key, w_value])
    spatial = (tokens, spatial_q, spatial_k, spatial_v, norm_gain)
    near_w = cross(own_w, 1)
    if by_ring:
        a = [own_w, turn(own_w)]
    mixed, own = spatial_call((me % 2).reshape(1), *spatial, None, CHUNKS)
    far = [cross(x, 2) for x in own]
    if by_ring:
        a.append(turn(after(a[1], own[0])))
    mixed, away = spatial_call((1 - me % 2).reshape(1), *spatial, mixed, CHUNKS)
    near = [cross(away[0], 1)]
    if by_ring:
        near_w = after(near_w, away[0])
        a[2] = after(a[2], away[0])
        a.append(turn(a[2]))
        near[0] = after(near[0], a[2])
    across = [cross(near[0], 2)]
    near.append(cross(after(away[1], near[0]), 1))
    if by_ring:
        a[3] = after(a[3], near[0])
        b = [near_w, turn(after(near_w, a[3]))]
        lent = cross(a[3], 1)
        b.append(turn(b[1]))
        b.append(lent)
        near[1] = after(near[1], b[1])
        groups = [w + [lax.ppermute(x, "view", swap) for x in w] for w in (a, b)]
        place = [(view - 2 * k) % n_view for k in range(n_view // 2)]
        place = [me] + place + [p ^ 1 for p in place]
    else:
        groups = [[lax.all_gather(w, "view", axis=1, tiled=True)] for w in (own_w, near_w)]
        place = [me, jnp.int32(0)]
    across.append(cross(near[1], 2))
    place = jnp.stack(place).astype(jnp.int32)
    attended = None
    for c in range(CHUNKS):
        xs = [own[c], near[c], far[c], across[c]]
        if c in SPLIT:
            outs = temporal_call(place, counts, xs, groups[0], [])
            outs = temporal_call(place, counts, xs, groups[1], outs)
        else:
            outs = temporal_call(place, counts, xs, groups[0] + groups[1], [])
        parts = [outs[0]] + [cross(outs[g], g) for g in range(1, n_tm)]
        attended = place_call(me.reshape(1), parts, attended, c, CHUNKS, size, width, n_tm * width)
    return (mixed, attended.reshape((1,) + attended.shape))


def solution(mesh):
    rows = P("view", "tm", None, None)
    in_specs = (rows, rows, rows, rows, P(), P("view", "tm"), P("view", "tm"), P("view", "tm"), P("view"))
    body = functools.partial(shards, mesh.shape["tm"], mesh.shape["view"])
    return jax.shard_map(body, mesh=mesh, in_specs=in_specs, out_specs=(rows, rows), check_vma=False)
```
